512 devices in a mesh: row: 16 (over z, core), col: 32 (over x, y).
Axes of the slice: x: 4, y: 8, z: 8, core: 2. Of those that a mesh axis runs over, the one named last changes fastest.
Arguments:
- lead: bfloat16 [2, 1024, 2048], P(None, 'row'), may hold values from -0.5 to 28, as said below
- panel: float32 [8192, 2048], P(('row', 'col')), may hold values from -6 to 6
- row_present: int32 [64], replicated, may hold values 0 or 1
- trailing: float32 [8192, 8192], P('row', 'col'), may hold values from -6 to 6
Outputs:
- updated: float32 [8192, 8192], P('row', 'col')
- factor_rows: bfloat16 [8192, 2048], P(('row', 'col'))
The draws below stay inside these ranges and needn't reach their ends.
Inputs may be any that keep to these rules, and one draw needn't show every extreme that they name: `lead`: the two halves stacked row after row form a symmetric positive definite matrix of order 2048.
All inputs are finite; a program needn't handle non-finite values.
Results may differ from the reference program's by a relative error of at most 0.0013.
Values may be sent and summed in bfloat16 or wider, within the bound.
A program may use at most 128 MiB of HBM per device.

```python
import jax
import jax.numpy as jnp
from jax import lax

PANEL = 1024
TILE = 128
LEAD = 2048
ROWS = 8192
TILES = 64


def draw_lead(key, part):
    key_band, key_far, key_diag, key_cross = jax.random.split(key, 4)
    positions = jnp.arange(LEAD)
    row_pos = positions[:, None]
    col_pos = positions[None, :]
    distance = jnp.abs(row_pos - col_pos)
    band_vals = jax.random.uniform(key_band, (LEAD, LEAD), jnp.float32, -0.5, 0.5)
    far_raw = jax.random.uniform(key_far, (LEAD, LEAD), jnp.float32, -1.0, 1.0)
    cross_vals = jax.random.uniform(key_cross, (LEAD, LEAD), jnp.float32, -0.3, 0.3)
    far_vals = far_raw * 0.1
    across = row_pos // PANEL != col_pos // PANEL
    outside = jnp.where(across, cross_vals, far_vals)
    offdiag = jnp.where(distance <= 8, band_vals, outside)
    symmetric = jnp.where(row_pos > col_pos, offdiag, offdiag.T)
    diag_vals = 22.0 + 6.0 * jax.random.uniform(key_diag, (LEAD,), jnp.float32)
    matrix = jnp.where(row_pos == col_pos, diag_vals[:, None], symmetric)
    return matrix.reshape(2, PANEL, LEAD).astype(jnp.bfloat16)


def place_ends(drawn, key, smallest, top_value):
    extent = drawn.shape
    spot = [jax.random.randint(jax.random.fold_in(key, axis), (), 0, extent[axis]) for axis in range(len(extent))]
    drawn = drawn.at[tuple(spot)].set(smallest)
    longest = extent.index(max(extent))
    spot[longest] = (spot[longest] + 1) % extent[longest]
    return drawn.at[tuple(spot)].set(top_value)


def steps_of(rng, dims, cuts, low, top_value):
    loudness, own = 1.0, jax.random.fold_in(rng, 6)
    for position, shards_of in cuts:
        heights = jnp.exp(jax.random.uniform(jax.random.fold_in(own, position), (shards_of,), jnp.float32, low / len(cuts), top_value / len(cuts)))
        loudness = loudness * jnp.repeat(heights, dims[position] // shards_of).reshape([-1 if axis == position else 1 for axis in range(len(dims))])
    return loudness


def scatter_about(own_key, extent, spread, most, cuts=(), held_as=jnp.bfloat16):
    result = jax.random.normal(own_key, extent, jnp.float32) * spread
    if len(cuts) > 0:
        result = steps_of(own_key, extent, cuts, -0.22, 0.18) * result
    return jnp.clip(result, min=-most, max=most).astype(held_as)


def setup_inputs(seed: int = 0) -> dict:
    key_of = jax.random.split(jax.random.key(seed), 5)
    return {
        "lead": draw_lead(jax.random.fold_in(key_of[4], 71), 0),
        "panel": scatter_about(key_of[1], (ROWS, LEAD), 1.0, 6.0, ((0, 512),), jnp.float32),
        "row_present": place_ends((jax.random.randint(key_of[2], (TILES,), 0, 4) < 3).astype(jnp.int32), jax.random.fold_in(key_of[2], 1), 0, 1),
        "trailing": scatter_about(key_of[3], (ROWS, ROWS), 1.0, 6.0, ((0, 16), (1, 32)), jnp.float32),
    }


def solve_right(factor, right_side):
    return lax.linalg.triangular_solve(factor, right_side, left_side=False, lower=True, transpose_a=True)

def reference(lead, panel, row_present, trailing):
    first_block = lead[0, :, :PANEL].astype(jnp.float32)
    first_factor = jnp.linalg.cholesky(first_block)
    coupling = solve_right(first_factor, lead[1, :, :PANEL].astype(jnp.float32)).astype(jnp.bfloat16)
    schur_block = lead[1, :, PANEL:].astype(jnp.float32) - jnp.dot(coupling.astype(jnp.float32), coupling.T.astype(jnp.float32), preferred_element_type=jnp.float32)
    second_factor = jnp.linalg.cholesky(schur_block)
    rowmask = jnp.repeat(row_present, TILE).astype(jnp.float32)
    masked = panel * rowmask[:, None]
    first_cols = solve_right(first_factor, masked[:, :PANEL]).astype(jnp.bfloat16)
    remainder = masked[:, PANEL:] - jnp.dot(first_cols.astype(jnp.float32), coupling.T.astype(jnp.float32), preferred_element_type=jnp.float32)
    second_cols = solve_right(second_factor, remainder).astype(jnp.bfloat16)
    factor_rows = jnp.concatenate([first_cols, second_cols], axis=1)
    updated = trailing - jnp.dot(factor_rows.astype(jnp.float32), factor_rows.T.astype(jnp.float32), preferred_element_type=jnp.float32)
    return (updated, factor_rows)
```

```python
import jax
import jax.numpy as jnp
from jax import lax
from jax.experimental import pallas as pl
from jax.experimental.pallas import tpu as pltpu
from jax.sharding import PartitionSpec as P

TILE = 128
F32 = jnp.float32
BF16 = jnp.bfloat16


def lane_cast(x, c):
    return jnp.broadcast_to(x[:, c : c + 1], (8, 128))


def sub_cast(x, j):
    return jnp.broadcast_to(x[j : j + 1, :], (8, 128))


def tree(xs):
    while len(xs) > 1:
        xs = [xs[i] + xs[i + 1] if i + 1 < len(xs) else xs[i] for i in range(0, len(xs), 2)]
    return xs[0]


def factor128(rows):
    lane = lax.broadcasted_iota(jnp.int32, (8, 128), 1)
    sub = lax.broadcasted_iota(jnp.int32, (8, 128), 0)
    rows = list(rows)
    out = []
    for k in range(16):
        c0 = 8 * k
        inside = (lane >= c0) & (lane < c0 + 8)
        casts = {r: [lane_cast(rows[r], c0 + c) for c in range(8)] for r in range(k, 16)}
        cols = list(casts[k])
        forward = jnp.where(inside, jnp.where(lane - c0 == sub, 1.0, 0.0), rows[k])
        full = forward
        recips = jnp.zeros((8, 128), F32)
        for j in range(8):
            recip = 1.0 / sub_cast(cols[j], j)
            mult = cols[j] * recip
            mult_full = jnp.where(sub == j, 0.0, mult)
            mult_fwd = jnp.where(sub > j, mult, 0.0)
            for c in range(j + 1, 8):
                cols[c] = cols[c] - mult_full * sub_cast(cols[c], j)
            full = full - mult_full * sub_cast(full, j)
            forward = forward - mult_fwd * sub_cast(forward, j)
            recips = jnp.where(sub == j, recip, recips)
        full = full * recips
        out.append(jnp.where(lane < c0 + 8, forward * lax.sqrt(recips), 0.0))
        pivots = [sub_cast(full, c) for c in range(8)]
        for r in range(k + 1, 16):
            rows[r] = jnp.where(inside, 0.0, rows[r]) - tree([casts[r][c] * pivots[c] for c in range(8)])
    return out


def split(x):
    hi = x.astype(BF16)
    return hi, (x - hi.astype(F32)).astype(BF16)


def split_outside(x):
    hi = lax.reduce_precision(x, 8, 7)
    return hi.astype(BF16), (x - hi).astype(BF16)


NN = (((1,), (0,)), ((), ()))
NT = (((1,), (1,)), ((), ()))


def dot(a, b, dims):
    return lax.dot_general(a, b, dims, preferred_element_type=F32)


def dot3(a, b, dims):
    return dot(a[0], b[0], dims) + (dot(a[0], b[1], dims) + dot(a[1], b[0], dims))


def inverse_factor_kernel(s_ref, x_ref, inv_ref, top_hi, top_lo, left_hi, left_lo):
    n = s_ref.shape[0]
    blocks = n // 128
    x_ref[...] = s_ref[...]
    column = lax.broadcasted_iota(jnp.int32, (128, n), 1)

    def step(j, carry):
        r0 = pl.multiple_of(j * 128, 128)
        here = pl.ds(r0, 128)
        rows = [x_ref[pl.ds(r0 + 8 * k, 8), here] for k in range(16)]
        for k, row in enumerate(factor128(rows)):
            inv_ref[8 * k : 8 * k + 8, :] = row
        inv = inv_ref[...]
        inv_parts = split(inv)
        top = dot3(inv_parts, split(x_ref[here, :]), NN)
        hi, lo = split(top)
        top_hi[...] = hi
        top_lo[...] = lo
        inv_hi, inv_lo = inv_parts
        top_hi[:, here] = inv_hi
        top_lo[:, here] = inv_lo
        left = dot3(split(x_ref[:, here]), inv_parts, NT)
        hi, lo = split(left)
        left_hi[...] = hi
        left_lo[...] = lo
        x_ref[here, :] = jnp.where(column < r0, top, 0.0)
        x_ref[here, here] = inv

        def below(i, inner):
            i0 = pl.multiple_of(i * 128, 128)
            at = pl.ds(i0, 128)
            take = dot3((left_hi[at, :], left_lo[at, :]), (top_hi[...], top_lo[...]), NN)
            x_ref[at, here] = jnp.zeros((128, 128), F32)
            x_ref[at, :] = x_ref[at, :] - take
            return inner

        lax.fori_loop(j + 1, blocks, below, 0)
        return carry

    lax.fori_loop(0, blocks, step, 0)


def inverse_factor(s):
    n = s.shape[0]
    return pl.pallas_call(
        inverse_factor_kernel,
        out_shape=jax.ShapeDtypeStruct((n, n), F32),
        in_specs=[pl.BlockSpec(memory_space=pltpu.VMEM)],
        out_specs=pl.BlockSpec(memory_space=pltpu.VMEM),
        scratch_shapes=[
            pltpu.VMEM((128, 128), F32),
            pltpu.VMEM((128, n), BF16),
            pltpu.VMEM((128, n), BF16),
            pltpu.VMEM((n, 128), BF16),
            pltpu.VMEM((n, 128), BF16),
        ],
        compiler_params=pltpu.CompilerParams(vmem_limit_bytes=40 << 20),
        cost_estimate=pl.CostEstimate(flops=40_000_000_000, bytes_accessed=8 << 20, transcendentals=0),
    )(s)


def on_device(lead, panel, row_present, trailing):
    half = lead.shape[2] // 2
    rows_n, cols_n = lax.axis_size("row"), lax.axis_size("col")
    row_id, col_id = lax.axis_index("row"), lax.axis_index("col")
    lead_all = gather_lead(lead, half)

    count = panel.shape[0]
    first_row = (row_id * cols_n + col_id) * count
    tile_of = (first_row + jnp.arange(count, dtype=jnp.int32)) // TILE
    hits = tile_of[:, None] == jnp.arange(row_present.shape[0], dtype=jnp.int32)[None, :]
    present = jnp.sum(jnp.where(hits, row_present[None, :], 0), axis=1).astype(F32)
    pieces = jnp.stack(split_outside(panel * present[:, None]))
    row_pieces = lax.all_gather(pieces, "col", axis=1, tiled=True)
    per_col = trailing.shape[1] // count
    pairs = []
    for r in range(rows_n):
        for c in range(cols_n):
            owner = c * per_col + r
            pairs.append((owner, r * cols_n + c))
    col_pieces = lax.ppermute(pieces, ("row", "col"), pairs)
    col_pieces = lax.all_gather(col_pieces, "row", axis=1, tiled=True)

    x1 = inverse_factor(lead_all[0].astype(F32))
    x1_parts = split_outside(x1)
    below = lead_all[1]
    coupling = (dot(below, x1_parts[0], NT) + dot(below, x1_parts[1], NT)).astype(BF16)
    schur = lead_all[2].astype(F32) - dot(coupling, coupling, NT)
    x2_parts = split_outside(inverse_factor(schur))

    def solve(parts):
        left = (parts[0, :, :half], parts[1, :, :half])
        first = dot3(left, x1_parts, NT).astype(BF16)
        right = parts[0, :, half:].astype(F32) + parts[1, :, half:].astype(F32)
        rest = split_outside(right - dot(first, coupling, NT))
        second = dot3(rest, x2_parts, NT).astype(BF16)
        return jnp.concatenate([first, second], axis=1)

    rows_all = solve(row_pieces)
    cols_all = solve(col_pieces)
    updated = trailing - dot(rows_all, cols_all, NT)
    factor_rows = lax.dynamic_slice_in_dim(rows_all, col_id * count, count, 0)
    return (updated, factor_rows)


def gather_lead(lead, half):
    out = []
    for which in (lead[0, :, :half], lead[1, :, :half], lead[1, :, half:]):
        out.append(lax.all_gather(which, "row", axis=0, tiled=True))
    return out


def solution(mesh):
    in_specs = (P(None, "row", None), P(("row", "col"), None), P(), P("row", "col"))
    out_specs = (P("row", "col"), P(("row", "col"), None))
    return jax.shard_map(
        on_device, mesh=mesh, in_specs=in_specs, out_specs=out_specs, check_vma=False
    )
```

```python
import jax
import jax.numpy as jnp
from jax import lax
from jax.experimental import pallas as pl
from jax.experimental.pallas import tpu as pltpu
from jax.sharding import PartitionSpec as P

TILE = 128
F32 = jnp.float32
BF16 = jnp.bfloat16


def lane_cast(x, c):
    return jnp.broadcast_to(x[:, c : c + 1], (8, 128))


def sub_cast(x, j):
    return jnp.broadcast_to(x[j : j + 1, :], (8, 128))


def tree(xs):
    while len(xs) > 1:
        xs = [xs[i] + xs[i + 1] if i + 1 < len(xs) else xs[i] for i in range(0, len(xs), 2)]
    return xs[0]


def factor128(rows):
    lane = lax.broadcasted_iota(jnp.int32, (8, 128), 1)
    sub = lax.broadcasted_iota(jnp.int32, (8, 128), 0)
    rows = list(rows)
    out = []
    for k in range(16):
        c0 = 8 * k
        inside = (lane >= c0) & (lane < c0 + 8)
        casts = {r: [lane_cast(rows[r], c0 + c) for c in range(8)] for r in range(k, 16)}
        cols = list(casts[k])
        forward = jnp.where(inside, jnp.where(lane - c0 == sub, 1.0, 0.0), rows[k])
        full = forward
        recips = jnp.zeros((8, 128), F32)
        for j in range(8):
            recip = 1.0 / sub_cast(cols[j], j)
            mult = cols[j] * recip
            mult_full = jnp.where(sub == j, 0.0, mult)
            mult_fwd = jnp.where(sub > j, mult, 0.0)
            for c in range(j + 1, 8):
                cols[c] = cols[c] - mult_full * sub_cast(cols[c], j)
            full = full - mult_full * sub_cast(full, j)
            forward = forward - mult_fwd * sub_cast(forward, j)
            recips = jnp.where(sub == j, recip, recips)
        full = full * recips
        out.append(jnp.where(lane < c0 + 8, forward * lax.sqrt(recips), 0.0))
        pivots = [sub_cast(full, c) for c in range(8)]
        for r in range(k + 1, 16):
            rows[r] = jnp.where(inside, 0.0, rows[r]) - tree([casts[r][c] * pivots[c] for c in range(8)])
    return out


def split(x):
    hi = x.astype(BF16)
    return hi, (x - hi.astype(F32)).astype(BF16)


def split_outside(x):
    hi = lax.reduce_precision(x, 8, 7)
    return hi.astype(BF16), (x - hi).astype(BF16)


NN = (((1,), (0,)), ((), ()))
NT = (((1,), (1,)), ((), ()))


def dot(a, b, dims):
    return lax.dot_general(a, b, dims, preferred_element_type=F32)


def dot3(a, b, dims):
    return dot(a[0], b[0], dims) + (dot(a[0], b[1], dims) + dot(a[1], b[0], dims))


def inverse_factor_kernel(s_ref, x_ref, *scratch):
    x_ref[...] = s_ref[...]
    invert_in_place(x_ref, *scratch)


def invert_in_place(x_ref, inv_ref, top_hi, top_lo, left_hi, left_lo):
    n = x_ref.shape[0]
    blocks = n // 128
    column = lax.broadcasted_iota(jnp.int32, (128, n), 1)

    def step(j, carry):
        r0 = pl.multiple_of(j * 128, 128)
        here = pl.ds(r0, 128)
        rows = [x_ref[pl.ds(r0 + 8 * k, 8), here] for k in range(16)]
        for k, row in enumerate(factor128(rows)):
            inv_ref[8 * k : 8 * k + 8, :] = row
        inv = inv_ref[...]
        inv_parts = split(inv)
        top = dot3(inv_parts, split(x_ref[here, :]), NN)
        hi, lo = split(top)
        top_hi[...] = hi
        top_lo[...] = lo
        inv_hi, inv_lo = inv_parts
        top_hi[:, here] = inv_hi
        top_lo[:, here] = inv_lo
        left = dot3(split(x_ref[:, here]), inv_parts, NT)
        hi, lo = split(left)
        left_hi[...] = hi
        left_lo[...] = lo
        x_ref[here, :] = jnp.where(column < r0, top, 0.0)
        x_ref[here, here] = inv

        def below(i, inner):
            i0 = pl.multiple_of(i * 128, 128)
            at = pl.ds(i0, 128)
            take = dot3((left_hi[at, :], left_lo[at, :]), (top_hi[...], top_lo[...]), NN)
            x_ref[at, here] = jnp.zeros((128, 128), F32)
            x_ref[at, :] = x_ref[at, :] - take
            return inner

        lax.fori_loop(j + 1, blocks, below, 0)
        return carry

    lax.fori_loop(0, blocks, step, 0)


def factor_scratch(n):
    return [
        pltpu.VMEM((128, 128), F32),
        pltpu.VMEM((128, n), BF16),
        pltpu.VMEM((128, n), BF16),
        pltpu.VMEM((n, 128), BF16),
        pltpu.VMEM((n, 128), BF16),
    ]


def inverse_factor(s):
    n = s.shape[0]
    return pl.pallas_call(
        inverse_factor_kernel,
        out_shape=jax.ShapeDtypeStruct((n, n), F32),
        in_specs=[pl.BlockSpec(memory_space=pltpu.VMEM)],
        out_specs=pl.BlockSpec(memory_space=pltpu.VMEM),
        scratch_shapes=factor_scratch(n),
        compiler_params=pltpu.CompilerParams(vmem_limit_bytes=40 << 20),
        cost_estimate=pl.CostEstimate(flops=40_000_000_000, bytes_accessed=8 << 20, transcendentals=0),
    )(s)


ZS, YS, XS = 8, 8, 4
MESH = pl.DeviceIdType.MESH


def lead_kernel(lead_ref, hi_ref, lo_ref, coupling_ref, schur_ref, buf, work, *scratch):
    factor_refs, (send_sem, recv_sem) = scratch[:5], scratch[5:]
    row, col = lax.axis_index("row"), lax.axis_index("col")
    z, core = row // 2, row % 2
    x, y = col // YS, col % YS
    half = lead_ref.shape[2] // 2

    peers = []
    for d in range(1, ZS):
        peers.append((lax.rem(z + d, ZS) * 2 + core, col))
    for d in range(1, YS):
        peers.append((row, x * YS + lax.rem(y + d, YS)))
    for d in range(1, XS):
        peers.append((row, lax.rem(x + d, XS) * YS + y))
    peers.append((z * 2 + 1 - core, col))

    barrier = pltpu.get_barrier_semaphore()
    for peer in peers:
        pl.semaphore_signal(barrier, inc=1, device_id=peer, device_id_type=MESH)

    high = pl.ds(pl.multiple_of(x * 16, 16), 16)
    wide = pl.ds(pl.multiple_of(y * 128, 128), 128)
    wide_right = pl.ds(pl.multiple_of(half + y * 128, 128), 128)
    buf[0, z, core, high, wide] = lead_ref[0, high, wide]
    buf[1, z, core, high, wide] = lead_ref[1, high, wide]
    buf[2, z, core, high, wide] = lead_ref[1, high, wide_right]
    pl.semaphore_wait(barrier, len(peers))

    def copies(group, phase, part):
        first, count = [(0, ZS - 1), (ZS - 1, YS - 1), (ZS + YS - 2, XS - 1), (ZS + YS + XS - 3, 1)][phase]
        return [
            pltpu.make_async_remote_copy(
                src_ref=part,
                dst_ref=part,
                send_sem=send_sem.at[group, first + n],
                recv_sem=recv_sem.at[group, first + n],
                device_id=peers[first + n],
                device_id_type=MESH,
            )
            for n in range(count)
        ]

    def phases(group, which):
        return [
            copies(group, 0, buf.at[which, z, core, high, wide]),
            copies(group, 1, buf.at[which, :, core, high, wide]),
            copies(group, 2, buf.at[which, :, core, high, :]),
            copies(group, 3, buf.at[which, :, core]),
        ]

    def start(cs):
        for c in cs:
            c.start()

    def wait(cs):
        for c in cs:
            c.wait()

    first = phases(0, pl.ds(0, 1))
    rest = phases(1, pl.ds(1, 2))
    start(first[0])
    start(rest[0])
    wait(first[0])
    start(first[1])
    wait(first[1])
    start(first[2])
    wait(rest[0])
    wait(first[2])
    start(first[3])
    start(rest[1])
    wait(first[3])
    work[...] = buf[0].reshape(work.shape).astype(F32)

    wait(rest[1])
    start(rest[2])
    invert_in_place(work, *factor_refs)
    wait(rest[2])
    start(rest[3])
    hi, lo = split(work[...])
    hi_ref[...] = hi
    lo_ref[...] = lo
    wait(rest[3])

    def coupling_rows(i, carry):
        at = pl.ds(pl.multiple_of(i * 128, 128), 128)
        left = buf[1, i].reshape(128, half)
        coupling_ref[at, :] = (dot(left, hi_ref[...], NT) + dot(left, lo_ref[...], NT)).astype(BF16)
        return carry

    lax.fori_loop(0, half // 128, coupling_rows, 0)

    def schur_rows(i, carry):
        at = pl.ds(pl.multiple_of(i * 128, 128), 128)
        schur_ref[at, :] = buf[2, i].reshape(128, half).astype(F32) - dot(coupling_ref[at, :], coupling_ref[...], NT)
        return carry

    lax.fori_loop(0, half // 128, schur_rows, 0)


def lead_factor(lead):
    half = lead.shape[2] // 2
    square = (half, half)
    vmem = pl.BlockSpec(memory_space=pltpu.VMEM)
    shapes = [(square, BF16), (square, BF16), (square, BF16), (square, F32)]
    return pl.pallas_call(
        lead_kernel,
        out_shape=[jax.ShapeDtypeStruct(s, t) for s, t in shapes],
        in_specs=[vmem],
        out_specs=[vmem] * 4,
        scratch_shapes=[
            pltpu.VMEM((3, ZS, 2, half // 16, half), BF16),
            pltpu.VMEM(square, F32),
            *factor_scratch(half),
            pltpu.SemaphoreType.DMA((2, ZS + YS + XS - 2)),
            pltpu.SemaphoreType.DMA((2, ZS + YS + XS - 2)),
        ],
        compiler_params=pltpu.CompilerParams(
            vmem_limit_bytes=48 << 20, collective_id=0, has_side_effects=True
        ),
        cost_estimate=pl.CostEstimate(flops=60_000_000_000, bytes_accessed=16 << 20, transcendentals=0),
    )(lead)


def on_device(lead, panel, row_present, trailing):
    half = lead.shape[2] // 2
    rows_n, cols_n = lax.axis_size("row"), lax.axis_size("col")
    row_id, col_id = lax.axis_index("row"), lax.axis_index("col")
    count = panel.shape[0]
    first_row = (row_id * cols_n + col_id) * count
    tile_of = (first_row + jnp.arange(count, dtype=jnp.int32)) // TILE
    hits = tile_of[:, None] == jnp.arange(row_present.shape[0], dtype=jnp.int32)[None, :]
    present = jnp.sum(jnp.where(hits, row_present[None, :], 0), axis=1).astype(F32)
    pieces = jnp.stack(split_outside(panel * present[:, None]))
    row_pieces = lax.all_gather(pieces, "col", axis=1, tiled=True)
    per_col = trailing.shape[1] // count
    pairs = []
    for r in range(rows_n):
        for c in range(cols_n):
            owner = c * per_col + r
            pairs.append((owner, r * cols_n + c))
    col_pieces = lax.ppermute(pieces, ("row", "col"), pairs)
    col_pieces = lax.all_gather(col_pieces, "row", axis=1, tiled=True)

    *x1_parts, coupling, schur = lead_factor(lead)
    x2_parts = split_outside(inverse_factor(schur))

    def solve(parts):
        left = (parts[0, :, :half], parts[1, :, :half])
        first = dot3(left, x1_parts, NT).astype(BF16)
        right = parts[0, :, half:].astype(F32) + parts[1, :, half:].astype(F32)
        rest = split_outside(right - dot(first, coupling, NT))
        second = dot3(rest, x2_parts, NT).astype(BF16)
        return jnp.concatenate([first, second], axis=1)

    rows_all = solve(row_pieces)
    cols_all = solve(col_pieces)
    updated = trailing - dot(rows_all, cols_all, NT)
    factor_rows = lax.dynamic_slice_in_dim(rows_all, col_id * count, count, 0)
    return (updated, factor_rows)


def solution(mesh):
    in_specs = (P(None, "row", None), P(("row", "col"), None), P(), P("row", "col"))
    out_specs = (P("row", "col"), P(("row", "col"), None))
    return jax.shard_map(
        on_device, mesh=mesh, in_specs=in_specs, out_specs=out_specs, check_vma=False
    )
```

```python
import jax
import jax.numpy as jnp
from jax import lax
from jax.experimental import pallas as pl
from jax.experimental.pallas import tpu as pltpu
from jax.sharding import PartitionSpec as P

TILE = 128
F32 = jnp.float32
BF16 = jnp.bfloat16


def lane_cast(x, c):
    return jnp.broadcast_to(x[:, c : c + 1], (8, 128))


def sub_cast(x, j):
    return jnp.broadcast_to(x[j : j + 1, :], (8, 128))


def tree(xs):
    while len(xs) > 1:
        xs = [xs[i] + xs[i + 1] if i + 1 < len(xs) else xs[i] for i in range(0, len(xs), 2)]
    return xs[0]


def factor128(rows):
    lane = lax.broadcasted_iota(jnp.int32, (8, 128), 1)
    sub = lax.broadcasted_iota(jnp.int32, (8, 128), 0)
    zero = jnp.zeros((8, 128), F32)
    rows = list(rows)
    out = []
    for k in range(0, 16, 2):
        c0 = 8 * k
        inside = (lane >= c0) & (lane < c0 + 16)
        casts = {r: [lane_cast(rows[r], c0 + c) for c in range(16)] for r in range(k, min(16, k + 4))}
        cols = [[casts[k][c], casts[k + 1][c]] for c in range(16)]
        forward = [jnp.where(inside, jnp.where(lane - c0 - 8 * i == sub, 1.0, 0.0), rows[k + i]) for i in range(2)]
        full = list(forward)
        recips = [zero, zero]
        for j in range(16):
            at, js = j // 8, j % 8
            recip = 1.0 / sub_cast(cols[j][at], js)
            mult = [cols[j][i] * recip for i in range(2)]
            below = [jnp.where(sub > js, mult[i], 0.0) if i == at else mult[i] for i in range(2)]
            mult[at] = jnp.where(sub == js, 0.0, mult[at])
            for c in range(j + 1, 16):
                pivot = sub_cast(cols[c][at], js)
                cols[c] = [cols[c][i] - mult[i] * pivot for i in range(2)]
            pivot = sub_cast(full[at], js)
            full = [full[i] - mult[i] * pivot for i in range(2)]
            pivot = sub_cast(forward[at], js)
            forward = [forward[i] - below[i] * pivot if i >= at else forward[i] for i in range(2)]
            recips[at] = jnp.where(sub == js, recip, recips[at])
        full = [full[i] * recips[i] for i in range(2)]
        for i in range(2):
            out.append(jnp.where(lane < c0 + 8 * i + 8, forward[i] * lax.sqrt(recips[i]), 0.0))
        pivots = [sub_cast(full[c // 8], c % 8) for c in range(16)]
        far = range(k + 4, 16)
        if len(far) > 0:
            step = split(jnp.concatenate([full[r - k] if k <= r < k + 2 else zero for r in range(16)], axis=0))
            take = dot3(split(jnp.concatenate([jnp.where(inside, rows[r], 0.0) for r in far], axis=0)), step, NN)
        for r in range(k + 2, 16):
            kept = jnp.where(inside, 0.0, rows[r])
            if r < k + 4:
                rows[r] = kept - tree([casts[r][c] * pivots[c] for c in range(16)])
            else:
                rows[r] = kept - take[8 * (r - k - 4) : 8 * (r - k - 4) + 8, :]
    return out


def split(x):
    hi = x.astype(BF16)
    return hi, (x - hi.astype(F32)).astype(BF16)


def split_outside(x):
    hi = lax.reduce_precision(x, 8, 7)
    return hi.astype(BF16), (x - hi).astype(BF16)


NN = (((1,), (0,)), ((), ()))
NT = (((1,), (1,)), ((), ()))


def dot(a, b, dims):
    return lax.dot_general(a, b, dims, preferred_element_type=F32)


def dot3(a, b, dims):
    return dot(a[0], b[0], dims) + (dot(a[0], b[1], dims) + dot(a[1], b[0], dims))


def invert_in_place(x_ref, inv_ref, top_hi, top_lo, left_hi, left_lo, before=None):
    n = x_ref.shape[0]
    blocks = n // 128
    column = lax.broadcasted_iota(jnp.int32, (128, n), 1)

    def step(j, carry):
        if before is not None:
            before(j)
        r0 = pl.multiple_of(j * 128, 128)
        here = pl.ds(r0, 128)
        rows = [x_ref[pl.ds(r0 + 8 * k, 8), here] for k in range(16)]
        for k, row in enumerate(factor128(rows)):
            inv_ref[8 * k : 8 * k + 8, :] = row
        inv = inv_ref[...]
        inv_parts = split(inv)
        top = dot3(inv_parts, split(x_ref[here, :]), NN)
        hi, lo = split(top)
        top_hi[...] = hi
        top_lo[...] = lo
        inv_hi, inv_lo = inv_parts
        top_hi[:, here] = inv_hi
        top_lo[:, here] = inv_lo
        left = dot3(split(x_ref[:, here]), inv_parts, NT)
        hi, lo = split(left)
        left_hi[...] = hi
        left_lo[...] = lo
        x_ref[here, :] = jnp.where(column < r0, top, 0.0)
        x_ref[here, here] = inv

        def below(i, inner):
            i0 = pl.multiple_of(i * 128, 128)
            at = pl.ds(i0, 128)
            take = dot3((left_hi[at, :], left_lo[at, :]), (top_hi[...], top_lo[...]), NN)
            x_ref[at, here] = jnp.zeros((128, 128), F32)
            x_ref[at, :] = x_ref[at, :] - take
            return inner

        lax.fori_loop(j + 1, blocks, below, 0)
        return carry

    lax.fori_loop(0, blocks, step, 0)


def factor_scratch(n):
    return [
        pltpu.VMEM((128, 128), F32),
        pltpu.VMEM((128, n), BF16),
        pltpu.VMEM((128, n), BF16),
        pltpu.VMEM((n, 128), BF16),
        pltpu.VMEM((n, 128), BF16),
    ]


ZS = 8
MESH = pl.DeviceIdType.MESH


def neighbours():
    row, col = lax.axis_index("row"), lax.axis_index("col")
    z, core = row // 2, row % 2
    up = (lax.rem(z + 1, ZS) * 2 + core, col)
    down = (lax.rem(z + ZS - 1, ZS) * 2 + core, col)
    return z, core, up, down, (z * 2 + 1 - core, col)


class Ring:
    def __init__(self, block_of, send_sem, recv_sem):
        z, core, up, down, other = neighbours()

        def copy(n, block, peer):
            part = block_of(lax.rem(block + ZS, ZS), core)
            return pltpu.make_async_remote_copy(
                src_ref=part,
                dst_ref=part,
                send_sem=send_sem.at[n],
                recv_sem=recv_sem.at[n],
                device_id=peer,
                device_id_type=MESH,
            )

        self.ups = [copy(n, z - n, up) for n in range(4)]
        self.downs = [copy(4 + n, z + n, down) for n in range(3)]
        self.across = [copy(7 + n, z - n, other) for n in range(5)]
        self.across += [copy(11 + n, z + n, other) for n in range(1, 4)]

    def begin(self):
        self.ups[0].start()
        self.downs[0].start()
        self.across[0].start()

    def advance(self, n):
        self.ups[n].wait_recv()
        if n < 3:
            self.ups[n + 1].start()
            self.downs[n].wait_recv()
        if n < 2:
            self.downs[n + 1].start()
        self.across[1 + n].start()
        if n < 3:
            self.across[5 + n].start()

    def finish(self):
        for c in self.across:
            c.wait()
        for c in self.ups + self.downs:
            c.wait_send()

    def advance_at(self, turns):
        def before(j):
            for n, turn in enumerate(turns):

                @pl.when(j == turn)
                def _():
                    self.advance(n)

        return before


def greet():
    barrier = pltpu.get_barrier_semaphore()
    for peer in neighbours()[2:]:
        pl.semaphore_signal(barrier, inc=1, device_id=peer, device_id_type=MESH)
    return barrier


def lead_kernel(lead_ref, hi_ref, lo_ref, coupling_ref, schur_ref, buf, work, *scratch):
    factor_refs, (send_sem, recv_sem) = scratch[:5], scratch[5:]
    z, core = neighbours()[:2]
    half = lead_ref.shape[2] // 2
    barrier = greet()
    buf[0, z, core] = lead_ref[0, :, :half]
    buf[1, z, core] = lead_ref[1, :, :half]
    buf[2, z, core] = lead_ref[1, :, half:]
    pl.semaphore_wait(barrier, 3)

    first = Ring(lambda b, c: buf.at[pl.ds(0, 1), b, c], send_sem.at[0], recv_sem.at[0])
    rest = Ring(lambda b, c: buf.at[pl.ds(1, 2), b, c], send_sem.at[1], recv_sem.at[1])
    first.begin()
    for n in range(4):
        first.advance(n)
    rest.begin()
    first.finish()
    work[...] = buf[0].reshape(work.shape).astype(F32)
    invert_in_place(work, *factor_refs, before=rest.advance_at((2, 4, 5, 7)))
    hi, lo = split(work[...])
    hi_ref[...] = hi
    lo_ref[...] = lo
    rest.finish()

    wide = 256
    for n in range(half // wide):
        at = slice(n * wide, n * wide + wide)
        depth = (n + 1) * wide
        left = buf[1, :, :, :, :depth].reshape(half, depth)
        coupling_ref[:, at] = (dot(left, hi_ref[at, :depth], NT) + dot(left, lo_ref[at, :depth], NT)).astype(BF16)

    def schur_columns(n, carry):
        at = pl.ds(pl.multiple_of(n * wide, wide), wide)
        block = buf[2, :, :, :, at].reshape(half, wide).astype(F32)
        schur_ref[:, at] = block - dot(coupling_ref[...], coupling_ref[at, :], NT)
        return carry

    lax.fori_loop(0, half // wide, schur_columns, 0)


def lead_factor(lead):
    half = lead.shape[2] // 2
    square = (half, half)
    vmem = pl.BlockSpec(memory_space=pltpu.VMEM)
    shapes = [(square, BF16)] * 3 + [(square, F32)]
    return pl.pallas_call(
        lead_kernel,
        out_shape=[jax.ShapeDtypeStruct(s, t) for s, t in shapes],
        in_specs=[vmem],
        out_specs=[vmem] * 4,
        scratch_shapes=[
            pltpu.VMEM((3, ZS, 2, half // 16, half), BF16),
            pltpu.VMEM(square, F32),
            *factor_scratch(half),
            pltpu.SemaphoreType.DMA((2, 15)),
            pltpu.SemaphoreType.DMA((2, 15)),
        ],
        compiler_params=pltpu.CompilerParams(
            vmem_limit_bytes=48 << 20, collective_id=0, has_side_effects=True
        ),
        cost_estimate=pl.CostEstimate(flops=6_000_000_000, bytes_accessed=16 << 20, transcendentals=0),
    )(lead)


def second_kernel(schur_ref, own_ref, hi_ref, lo_ref, cols_ref, work, *scratch):
    factor_refs, (send_sem, recv_sem) = scratch[:5], scratch[5:]
    z, core = neighbours()[:2]
    barrier = greet()
    cols_ref[z, core] = own_ref[...]
    work[...] = schur_ref[...]
    pl.semaphore_wait(barrier, 3)
    ring = Ring(lambda b, c: cols_ref.at[b, c], send_sem, recv_sem)
    ring.begin()
    invert_in_place(work, *factor_refs, before=ring.advance_at((1, 2, 3, 4)))
    hi, lo = split(work[...])
    hi_ref[...] = hi
    lo_ref[...] = lo
    ring.finish()


def second_factor(schur, own):
    n = schur.shape[0]
    vmem = pl.BlockSpec(memory_space=pltpu.VMEM)
    shapes = [(n, n), (n, n), (ZS, 2, *own.shape)]
    return pl.pallas_call(
        second_kernel,
        out_shape=[jax.ShapeDtypeStruct(s, BF16) for s in shapes],
        in_specs=[vmem] * 2,
        out_specs=[vmem] * 3,
        scratch_shapes=[
            pltpu.VMEM((n, n), F32),
            *factor_scratch(n),
            pltpu.SemaphoreType.DMA((15,)),
            pltpu.SemaphoreType.DMA((15,)),
        ],
        compiler_params=pltpu.CompilerParams(
            vmem_limit_bytes=48 << 20, collective_id=1, has_side_effects=True
        ),
        cost_estimate=pl.CostEstimate(flops=4_000_000_000, bytes_accessed=8 << 20, transcendentals=0),
    )(schur, own)


def on_device(lead, panel, row_present, trailing):
    half = lead.shape[2] // 2
    rows_n, cols_n = lax.axis_size("row"), lax.axis_size("col")
    row_id, col_id = lax.axis_index("row"), lax.axis_index("col")
    count = panel.shape[0]
    first_row = (row_id * cols_n + col_id) * count
    tile_of = (first_row + jnp.arange(count, dtype=jnp.int32)) // TILE
    hits = tile_of[:, None] == jnp.arange(row_present.shape[0], dtype=jnp.int32)[None, :]
    present = jnp.sum(jnp.where(hits, row_present[None, :], 0), axis=1).astype(F32)
    masked = panel * present[:, None]
    per_col = trailing.shape[1] // count
    pairs = []
    for r in range(rows_n):
        for c in range(cols_n):
            pairs.append((c * per_col + r, r * cols_n + c))

    hi, lo = split_outside(masked)
    pieces = jnp.stack([hi, lo])
    row_pieces = lax.all_gather(pieces, "col", axis=1, tiled=True)
    mine = jnp.concatenate([hi[:, :half], lo[:, :half], hi[:, half:], lo[:, half:]], axis=0)
    mine = lax.ppermute(mine, ("row", "col"), pairs)
    *x1_parts, coupling, schur = lead_factor(lead)
    *x2_parts, col_pieces = second_factor(schur, mine)
    col_pieces = col_pieces.reshape(rows_n, 4, count, half)
    col_parts = [col_pieces[:, n].reshape(rows_n * count, half) for n in range(4)]

    def solve(left_hi, left_lo, right_hi, right_lo):
        first = dot3((left_hi, left_lo), x1_parts, NT).astype(BF16)
        whole = right_hi.astype(F32) + right_lo.astype(F32)
        rest = split_outside(whole - dot(first, coupling, NT))
        second = dot3(rest, x2_parts, NT).astype(BF16)
        return jnp.concatenate([first, second], axis=1)

    row_hi, row_lo = row_pieces
    rows_all = solve(row_hi[:, :half], row_lo[:, :half], row_hi[:, half:], row_lo[:, half:])
    cols_all = solve(*col_parts)
    updated = trailing - dot(rows_all, cols_all, NT)
    factor_rows = lax.dynamic_slice_in_dim(rows_all, col_id * count, count, 0)
    return (updated, factor_rows)


def solution(mesh):
    in_specs = (P(None, "row", None), P(("row", "col"), None), P(), P("row", "col"))
    out_specs = (P("row", "col"), P(("row", "col"), None))
    return jax.shard_map(
        on_device, mesh=mesh, in_specs=in_specs, out_specs=out_specs, check_vma=False
    )
```

```python
import jax
import jax.numpy as jnp
from jax import lax
from jax.experimental import pallas as pl
from jax.experimental.pallas import tpu as pltpu
from jax.sharding import PartitionSpec as P

TILE = 128
F32 = jnp.float32
BF16 = jnp.bfloat16


def lane_cast(x, c):
    return jnp.broadcast_to(x[:, c : c + 1], (8, 128))


def sub_cast(x, j):
    return jnp.broadcast_to(x[j : j + 1, :], (8, 128))


def tree(xs):
    while len(xs) > 1:
        xs = [xs[i] + xs[i + 1] if i + 1 < len(xs) else xs[i] for i in range(0, len(xs), 2)]
    return xs[0]


def factor128(rows):
    lane = lax.broadcasted_iota(jnp.int32, (8, 128), 1)
    sub = lax.broadcasted_iota(jnp.int32, (8, 128), 0)
    zero = jnp.zeros((8, 128), F32)
    rows = list(rows)
    out = []
    for k in range(0, 16, 2):
        c0 = 8 * k
        inside = (lane >= c0) & (lane < c0 + 16)
        casts = {r: [lane_cast(rows[r], c0 + c) for c in range(16)] for r in range(k, min(16, k + 4))}
        cols = [[casts[k][c], casts[k + 1][c]] for c in range(16)]
        forward = [jnp.where(inside, jnp.where(lane - c0 - 8 * i == sub, 1.0, 0.0), rows[k + i]) for i in range(2)]
        full = list(forward)
        recips = [zero, zero]
        for j in range(16):
            at, js = j // 8, j % 8
            recip = 1.0 / sub_cast(cols[j][at], js)
            mult = [cols[j][i] * recip for i in range(2)]
            below = [jnp.where(sub > js, mult[i], 0.0) if i == at else mult[i] for i in range(2)]
            mult[at] = jnp.where(sub == js, 0.0, mult[at])
            for c in range(j + 1, 16):
                pivot = sub_cast(cols[c][at], js)
                cols[c] = [cols[c][i] - mult[i] * pivot for i in range(2)]
            pivot = sub_cast(full[at], js)
            full = [full[i] - mult[i] * pivot for i in range(2)]
            pivot = sub_cast(forward[at], js)
            forward = [forward[i] - below[i] * pivot if i >= at else forward[i] for i in range(2)]
            recips[at] = jnp.where(sub == js, recip, recips[at])
        full = [full[i] * recips[i] for i in range(2)]
        for i in range(2):
            out.append(jnp.where(lane < c0 + 8 * i + 8, forward[i] * lax.sqrt(recips[i]), 0.0))
        pivots = [sub_cast(full[c // 8], c % 8) for c in range(16)]
        far = range(k + 4, 16)
        if len(far) > 0:
            step = split(jnp.concatenate([full[r - k] if k <= r < k + 2 else zero for r in range(16)], axis=0))
            take = dot3(split(jnp.concatenate([jnp.where(inside, rows[r], 0.0) for r in far], axis=0)), step, NN)
        for r in range(k + 2, 16):
            kept = jnp.where(inside, 0.0, rows[r])
            if r < k + 4:
                rows[r] = kept - tree([casts[r][c] * pivots[c] for c in range(16)])
            else:
                rows[r] = kept - take[8 * (r - k - 4) : 8 * (r - k - 4) + 8, :]
    return out


def split(x):
    hi = x.astype(BF16)
    return hi, (x - hi.astype(F32)).astype(BF16)


def split_outside(x):
    hi = lax.reduce_precision(x, 8, 7)
    return hi.astype(BF16), (x - hi).astype(BF16)


NN = (((1,), (0,)), ((), ()))
NT = (((1,), (1,)), ((), ()))


def dot(a, b, dims):
    return lax.dot_general(a, b, dims, preferred_element_type=F32)


def dot3(a, b, dims):
    return dot(a[0], b[0], dims) + (dot(a[0], b[1], dims) + dot(a[1], b[0], dims))


def invert_in_place(x_ref, inv_ref, top_hi, top_lo, left_hi, left_lo, before=None):
    n = x_ref.shape[0]
    blocks = n // 128
    column = lax.broadcasted_iota(jnp.int32, (128, n), 1)

    def step(j, carry):
        if before is not None:
            before(j)
        r0 = pl.multiple_of(j * 128, 128)
        here = pl.ds(r0, 128)
        rows = [x_ref[pl.ds(r0 + 8 * k, 8), here] for k in range(16)]
        for k, row in enumerate(factor128(rows)):
            inv_ref[8 * k : 8 * k + 8, :] = row
        inv = inv_ref[...]
        inv_parts = split(inv)
        top = dot3(inv_parts, split(x_ref[here, :]), NN)
        hi, lo = split(top)
        top_hi[...] = hi
        top_lo[...] = lo
        inv_hi, inv_lo = inv_parts
        top_hi[:, here] = inv_hi
        top_lo[:, here] = inv_lo
        left = dot3(split(x_ref[:, here]), inv_parts, NT)
        hi, lo = split(left)
        left_hi[...] = hi
        left_lo[...] = lo
        x_ref[here, :] = jnp.where(column < r0, top, 0.0)
        x_ref[here, here] = inv

        def below(i, inner):
            i0 = pl.multiple_of(i * 128, 128)
            at = pl.ds(i0, 128)
            take = dot3((left_hi[at, :], left_lo[at, :]), (top_hi[...], top_lo[...]), NN)
            x_ref[at, here] = jnp.zeros((128, 128), F32)
            x_ref[at, :] = x_ref[at, :] - take
            return inner

        lax.fori_loop(j + 1, blocks, below, 0)
        return carry

    lax.fori_loop(0, blocks, step, 0)


def factor_scratch(n):
    return [
        pltpu.VMEM((128, 128), F32),
        pltpu.VMEM((128, n), BF16),
        pltpu.VMEM((128, n), BF16),
        pltpu.VMEM((n, 128), BF16),
        pltpu.VMEM((n, 128), BF16),
    ]


ZS = 8
MESH = pl.DeviceIdType.MESH


def neighbours():
    row, col = lax.axis_index("row"), lax.axis_index("col")
    z, core = row // 2, row % 2
    up = (lax.rem(z + 1, ZS) * 2 + core, col)
    down = (lax.rem(z + ZS - 1, ZS) * 2 + core, col)
    return z, core, up, down, (z * 2 + 1 - core, col)


class Ring:
    def __init__(self, block_of, send_sem, recv_sem):
        z, core, up, down, other = neighbours()

        def copy(n, block, peer):
            part = block_of(lax.rem(block + ZS, ZS), core)
            return pltpu.make_async_remote_copy(
                src_ref=part,
                dst_ref=part,
                send_sem=send_sem.at[n],
                recv_sem=recv_sem.at[n],
                device_id=peer,
                device_id_type=MESH,
            )

        self.ups = [copy(n, z - n, up) for n in range(4)]
        self.downs = [copy(4 + n, z + n, down) for n in range(3)]
        self.across = [copy(7 + n, z - n, other) for n in range(5)]
        self.across += [copy(11 + n, z + n, other) for n in range(1, 4)]

    def begin(self):
        self.ups[0].start()
        self.downs[0].start()
        self.across[0].start()

    def advance(self, n):
        self.ups[n].wait_recv()
        if n < 3:
            self.ups[n + 1].start()
            self.downs[n].wait_recv()
        if n < 2:
            self.downs[n + 1].start()
        self.across[1 + n].start()
        if n < 3:
            self.across[5 + n].start()

    def finish(self):
        for c in self.across:
            c.wait()
        for c in self.ups + self.downs:
            c.wait_send()

    def advance_at(self, turns):
        def before(j):
            for n, turn in enumerate(turns):

                @pl.when(j == turn)
                def _():
                    self.advance(n)

        return before


def greet():
    barrier = pltpu.get_barrier_semaphore()
    for peer in neighbours()[2:]:
        pl.semaphore_signal(barrier, inc=1, device_id=peer, device_id_type=MESH)
    return barrier


def lead_kernel(lead_ref, hi_ref, lo_ref, coupling_ref, buf, work, *scratch):
    factor_refs, (send_sem, recv_sem) = scratch[:5], scratch[5:]
    z, core = neighbours()[:2]
    half = lead_ref.shape[2] // 2
    barrier = greet()
    buf[0, z, core] = lead_ref[0, :, :half]
    buf[1, z, core] = lead_ref[1, :, :half]
    pl.semaphore_wait(barrier, 3)

    first = Ring(lambda b, c: buf.at[0, b, c], send_sem.at[0], recv_sem.at[0])
    rest = Ring(lambda b, c: buf.at[1, b, c], send_sem.at[1], recv_sem.at[1])
    first.begin()
    for n in range(4):
        first.advance(n)
    rest.begin()
    first.finish()
    work[...] = buf[0].reshape(work.shape).astype(F32)
    invert_in_place(work, *factor_refs, before=rest.advance_at((2, 3, 5, 6)))
    hi, lo = split(work[...])
    hi_ref[...] = hi
    lo_ref[...] = lo
    rest.finish()

    wide = 256
    for n in range(half // wide):
        at = slice(n * wide, n * wide + wide)
        depth = (n + 1) * wide
        left = buf[1, :, :, :, :depth].reshape(half, depth)
        coupling_ref[:, at] = (dot(left, hi_ref[at, :depth], NT) + dot(left, lo_ref[at, :depth], NT)).astype(BF16)


def lead_factor(lead):
    half = lead.shape[2] // 2
    square = (half, half)
    vmem = pl.BlockSpec(memory_space=pltpu.VMEM)
    shapes = [(square, BF16)] * 3
    return pl.pallas_call(
        lead_kernel,
        out_shape=[jax.ShapeDtypeStruct(s, t) for s, t in shapes],
        in_specs=[vmem],
        out_specs=[vmem] * 3,
        scratch_shapes=[
            pltpu.VMEM((2, ZS, 2, half // 16, half), BF16),
            pltpu.VMEM(square, F32),
            *factor_scratch(half),
            pltpu.SemaphoreType.DMA((2, 15)),
            pltpu.SemaphoreType.DMA((2, 15)),
        ],
        compiler_params=pltpu.CompilerParams(
            vmem_limit_bytes=48 << 20, collective_id=0, has_side_effects=True
        ),
        cost_estimate=pl.CostEstimate(flops=6_000_000_000, bytes_accessed=16 << 20, transcendentals=0),
    )(lead)


def second_kernel(corner_ref, coupling_ref, own_ref, hi_ref, lo_ref, cols_ref, work, *scratch):
    factor_refs, (send_sem, recv_sem) = scratch[:5], scratch[5:]
    z, core = neighbours()[:2]
    barrier = greet()
    cols_ref[z, core] = own_ref[...]
    pl.semaphore_wait(barrier, 3)
    ring = Ring(lambda b, c: cols_ref.at[b, c], send_sem, recv_sem)
    ring.begin()
    wide = 256

    def schur_columns(n, carry):
        at = pl.ds(pl.multiple_of(n * wide, wide), wide)
        work[:, at] = corner_ref[:, at].astype(F32) - dot(coupling_ref[...], coupling_ref[at, :], NT)
        return carry

    lax.fori_loop(0, work.shape[0] // wide, schur_columns, 0)
    invert_in_place(work, *factor_refs, before=ring.advance_at((1, 2, 3, 4)))
    hi, lo = split(work[...])
    hi_ref[...] = hi
    lo_ref[...] = lo
    ring.finish()


def second_factor(corner, coupling, own):
    n = corner.shape[0]
    vmem = pl.BlockSpec(memory_space=pltpu.VMEM)
    shapes = [(n, n), (n, n), (ZS, 2, *own.shape)]
    return pl.pallas_call(
        second_kernel,
        out_shape=[jax.ShapeDtypeStruct(s, BF16) for s in shapes],
        in_specs=[vmem] * 3,
        out_specs=[vmem] * 3,
        scratch_shapes=[
            pltpu.VMEM((n, n), F32),
            *factor_scratch(n),
            pltpu.SemaphoreType.DMA((15,)),
            pltpu.SemaphoreType.DMA((15,)),
        ],
        compiler_params=pltpu.CompilerParams(
            vmem_limit_bytes=48 << 20, collective_id=1, has_side_effects=True
        ),
        cost_estimate=pl.CostEstimate(flops=4_000_000_000, bytes_accessed=8 << 20, transcendentals=0),
    )(corner, coupling, own)


def on_device(lead, panel, row_present, trailing):
    half = lead.shape[2] // 2
    rows_n, cols_n = lax.axis_size("row"), lax.axis_size("col")
    row_id, col_id = lax.axis_index("row"), lax.axis_index("col")
    corner = lax.all_gather(lead[1, :, half:], "row", axis=0, tiled=True)
    count = panel.shape[0]
    first_row = (row_id * cols_n + col_id) * count
    tile_of = (first_row + jnp.arange(count, dtype=jnp.int32)) // TILE
    hits = tile_of[:, None] == jnp.arange(row_present.shape[0], dtype=jnp.int32)[None, :]
    present = jnp.sum(jnp.where(hits, row_present[None, :], 0), axis=1).astype(F32)
    masked = panel * present[:, None]
    per_col = trailing.shape[1] // count
    pairs = []
    for r in range(rows_n):
        for c in range(cols_n):
            pairs.append((c * per_col + r, r * cols_n + c))

    hi, lo = split_outside(masked)
    four = [hi[:, :half], lo[:, :half], hi[:, half:], lo[:, half:]]
    row_pieces = lax.all_gather(jnp.stack(four), "col", axis=1, tiled=True)
    mine = lax.ppermute(jnp.concatenate(four, axis=0), ("row", "col"), pairs)
    *x1_parts, coupling = lead_factor(lead)
    *x2_parts, col_pieces = second_factor(corner, coupling, mine)
    col_pieces = col_pieces.reshape(rows_n, 4, count, half)
    col_parts = [col_pieces[:, n].reshape(rows_n * count, half) for n in range(4)]

    def solve(left_hi, left_lo, right_hi, right_lo):
        first = dot3((left_hi, left_lo), x1_parts, NT).astype(BF16)
        whole = right_hi.astype(F32) + right_lo.astype(F32)
        rest = split_outside(whole - dot(first, coupling, NT))
        second = dot3(rest, x2_parts, NT).astype(BF16)
        return jnp.concatenate([first, second], axis=1)

    rows_all = solve(*[row_pieces[n] for n in range(4)])
    cols_all = solve(*col_parts)
    updated = trailing - dot(rows_all, cols_all, NT)
    factor_rows = lax.dynamic_slice_in_dim(rows_all, col_id * count, count, 0)
    return (updated, factor_rows)


def solution(mesh):
    in_specs = (P(None, "row", None), P(("row", "col"), None), P(), P("row", "col"))
    out_specs = (P("row", "col"), P(("row", "col"), None))
    return jax.shard_map(
        on_device, mesh=mesh, in_specs=in_specs, out_specs=out_specs, check_vma=False
    )
```

```python
import jax
import jax.numpy as jnp
from jax import lax
from jax.experimental import pallas as pl
from jax.experimental.pallas import tpu as pltpu
from jax.sharding import PartitionSpec as P

TILE = 128
F32 = jnp.float32
BF16 = jnp.bfloat16


def lane_cast(x, c):
    return jnp.broadcast_to(x[:, c : c + 1], (8, 128))


def sub_cast(x, j):
    return jnp.broadcast_to(x[j : j + 1, :], (8, 128))


def tree(xs):
    while len(xs) > 1:
        xs = [xs[i] + xs[i + 1] if i + 1 < len(xs) else xs[i] for i in range(0, len(xs), 2)]
    return xs[0]


def factor128(rows):
    lane = lax.broadcasted_iota(jnp.int32, (8, 128), 1)
    sub = lax.broadcasted_iota(jnp.int32, (8, 128), 0)
    zero = jnp.zeros((8, 128), F32)
    rows = list(rows)
    out = []
    for k in range(0, 16, 2):
        c0 = 8 * k
        inside = (lane >= c0) & (lane < c0 + 16)
        casts = {r: [lane_cast(rows[r], c0 + c) for c in range(16)] for r in range(k, min(16, k + 4))}
        cols = [[casts[k][c], casts[k + 1][c]] for c in range(16)]
        forward = [jnp.where(inside, jnp.where(lane - c0 - 8 * i == sub, 1.0, 0.0), rows[k + i]) for i in range(2)]
        full = list(forward)
        recips = [zero, zero]
        for j in range(16):
            at, js = j // 8, j % 8
            recip = 1.0 / sub_cast(cols[j][at], js)
            mult = [cols[j][i] * recip for i in range(2)]
            below = [jnp.where(sub > js, mult[i], 0.0) if i == at else mult[i] for i in range(2)]
            mult[at] = jnp.where(sub == js, 0.0, mult[at])
            for c in range(j + 1, 16):
                pivot = sub_cast(cols[c][at], js)
                cols[c] = [cols[c][i] - mult[i] * pivot for i in range(2)]
            pivot = sub_cast(full[at], js)
            full = [full[i] - mult[i] * pivot for i in range(2)]
            pivot = sub_cast(forward[at], js)
            forward = [forward[i] - below[i] * pivot if i >= at else forward[i] for i in range(2)]
            recips[at] = jnp.where(sub == js, recip, recips[at])
        full = [full[i] * recips[i] for i in range(2)]
        for i in range(2):
            out.append(jnp.where(lane < c0 + 8 * i + 8, forward[i] * lax.sqrt(recips[i]), 0.0))
        pivots = [sub_cast(full[c // 8], c % 8) for c in range(16)]
        far = range(k + 4, 16)
        if len(far) > 0:
            step = split(jnp.concatenate([full[r - k] if k <= r < k + 2 else zero for r in range(16)], axis=0))
            take = dot3(split(jnp.concatenate([jnp.where(inside, rows[r], 0.0) for r in far], axis=0)), step, NN)
        for r in range(k + 2, 16):
            kept = jnp.where(inside, 0.0, rows[r])
            if r < k + 4:
                rows[r] = kept - tree([casts[r][c] * pivots[c] for c in range(16)])
            else:
                rows[r] = kept - take[8 * (r - k - 4) : 8 * (r - k - 4) + 8, :]
    return out


def split(x):
    hi = x.astype(BF16)
    return hi, (x - hi.astype(F32)).astype(BF16)


def split_outside(x):
    hi = lax.reduce_precision(x, 8, 7)
    return hi.astype(BF16), (x - hi).astype(BF16)


NN = (((1,), (0,)), ((), ()))
NT = (((1,), (1,)), ((), ()))


def dot(a, b, dims):
    return lax.dot_general(a, b, dims, preferred_element_type=F32)


def dot3(a, b, dims):
    return dot(a[0], b[0], dims) + (dot(a[0], b[1], dims) + dot(a[1], b[0], dims))


def invert_in_place(x_ref, inv_ref, top_hi, top_lo, left_hi, left_lo, before=None):
    n = x_ref.shape[0]
    blocks = n // 128
    column = lax.broadcasted_iota(jnp.int32, (128, n), 1)

    def step(j, carry):
        if before is not None:
            before(j)
        r0 = pl.multiple_of(j * 128, 128)
        here = pl.ds(r0, 128)
        rows = [x_ref[pl.ds(r0 + 8 * k, 8), here] for k in range(16)]
        for k, row in enumerate(factor128(rows)):
            inv_ref[8 * k : 8 * k + 8, :] = row
        inv = inv_ref[...]
        inv_parts = split(inv)
        top = dot3(inv_parts, split(x_ref[here, :]), NN)
        hi, lo = split(top)
        top_hi[...] = hi
        top_lo[...] = lo
        inv_hi, inv_lo = inv_parts
        top_hi[:, here] = inv_hi
        top_lo[:, here] = inv_lo
        left = dot3(split(x_ref[:, here]), inv_parts, NT)
        hi, lo = split(left)
        left_hi[...] = hi
        left_lo[...] = lo
        x_ref[here, :] = jnp.where(column < r0, top, 0.0)
        x_ref[here, here] = inv

        def below(i, inner):
            i0 = pl.multiple_of(i * 128, 128)
            at = pl.ds(i0, 128)
            take = dot3((left_hi[at, :], left_lo[at, :]), (top_hi[...], top_lo[...]), NN)
            x_ref[at, here] = jnp.zeros((128, 128), F32)
            x_ref[at, :] = x_ref[at, :] - take
            return inner

        lax.fori_loop(j + 1, blocks, below, 0)
        return carry

    lax.fori_loop(0, blocks, step, 0)


def factor_scratch(n):
    return [
        pltpu.VMEM((128, 128), F32),
        pltpu.VMEM((128, n), BF16),
        pltpu.VMEM((128, n), BF16),
        pltpu.VMEM((n, 128), BF16),
        pltpu.VMEM((n, 128), BF16),
    ]


ZS = 8
MESH = pl.DeviceIdType.MESH


def neighbours():
    row, col = lax.axis_index("row"), lax.axis_index("col")
    z, core = row // 2, row % 2
    up = (lax.rem(z + 1, ZS) * 2 + core, col)
    down = (lax.rem(z + ZS - 1, ZS) * 2 + core, col)
    return z, core, up, down, (z * 2 + 1 - core, col)


class Ring:
    def __init__(self, block_of, send_sem, recv_sem):
        z, core, up, down, other = neighbours()

        def copy(n, block, peer):
            part = block_of(lax.rem(block + ZS, ZS), core)
            return pltpu.make_async_remote_copy(
                src_ref=part,
                dst_ref=part,
                send_sem=send_sem.at[n],
                recv_sem=recv_sem.at[n],
                device_id=peer,
                device_id_type=MESH,
            )

        self.ups = [copy(n, z - n, up) for n in range(4)]
        self.downs = [copy(4 + n, z + n, down) for n in range(3)]
        self.across = [copy(7 + n, z - n, other) for n in range(5)]
        self.across += [copy(11 + n, z + n, other) for n in range(1, 4)]

    def begin(self):
        self.ups[0].start()
        self.downs[0].start()
        self.across[0].start()

    def advance(self, n):
        self.ups[n].wait_recv()
        if n < 3:
            self.ups[n + 1].start()
            self.downs[n].wait_recv()
        if n < 2:
            self.downs[n + 1].start()
        self.across[1 + n].start()
        if n < 3:
            self.across[5 + n].start()

    def finish(self):
        for c in self.across:
            c.wait()
        for c in self.ups + self.downs:
            c.wait_send()

    def advance_at(self, turns):
        def before(j):
            for n, turn in enumerate(turns):

                @pl.when(j == turn)
                def _():
                    self.advance(n)

        return before


def greet():
    barrier = pltpu.get_barrier_semaphore()
    for peer in neighbours()[2:]:
        pl.semaphore_signal(barrier, inc=1, device_id=peer, device_id_type=MESH)
    return barrier


def lead_kernel(lead_ref, hi_ref, lo_ref, coupling_ref, schur_ref, buf, work, *scratch):
    factor_refs, (send_sem, recv_sem) = scratch[:5], scratch[5:]
    z, core = neighbours()[:2]
    half = lead_ref.shape[2] // 2
    barrier = greet()
    buf[0, z, core] = lead_ref[0, :, :half]
    buf[1, z, core] = lead_ref[1, :, :half]
    buf[2, z, core] = lead_ref[1, :, half:]
    pl.semaphore_wait(barrier, 3)

    first = Ring(lambda b, c: buf.at[pl.ds(0, 1), b, c], send_sem.at[0], recv_sem.at[0])
    rest = Ring(lambda b, c: buf.at[pl.ds(1, 2), b, c], send_sem.at[1], recv_sem.at[1])
    first.begin()
    for n in range(4):
        first.advance(n)
    rest.begin()
    first.finish()
    work[...] = buf[0].reshape(work.shape).astype(F32)
    invert_in_place(work, *factor_refs, before=rest.advance_at((2, 4, 5, 7)))
    hi, lo = split(work[...])
    hi_ref[...] = hi
    lo_ref[...] = lo
    rest.finish()

    wide = 256
    for n in range(half // wide):
        at = slice(n * wide, n * wide + wide)
        depth = (n + 1) * wide
        left = buf[1, :, :, :, :depth].reshape(half, depth)
        coupling_ref[:, at] = (dot(left, hi_ref[at, :depth], NT) + dot(left, lo_ref[at, :depth], NT)).astype(BF16)

    def schur_columns(n, carry):
        at = pl.ds(pl.multiple_of(n * wide, wide), wide)
        block = buf[2, :, :, :, at].reshape(half, wide).astype(F32)
        schur_ref[:, at] = block - dot(coupling_ref[...], coupling_ref[at, :], NT)
        return carry

    lax.fori_loop(0, half // wide, schur_columns, 0)


def lead_factor(lead):
    half = lead.shape[2] // 2
    square = (half, half)
    vmem = pl.BlockSpec(memory_space=pltpu.VMEM)
    shapes = [(square, BF16)] * 3 + [(square, F32)]
    return pl.pallas_call(
        lead_kernel,
        out_shape=[jax.ShapeDtypeStruct(s, t) for s, t in shapes],
        in_specs=[vmem],
        out_specs=[vmem] * 4,
        scratch_shapes=[
            pltpu.VMEM((3, ZS, 2, half // 16, half), BF16),
            pltpu.VMEM(square, F32),
            *factor_scratch(half),
            pltpu.SemaphoreType.DMA((2, 15)),
            pltpu.SemaphoreType.DMA((2, 15)),
        ],
        compiler_params=pltpu.CompilerParams(
            vmem_limit_bytes=48 << 20, collective_id=0, has_side_effects=True
        ),
        cost_estimate=pl.CostEstimate(flops=6_000_000_000, bytes_accessed=16 << 20, transcendentals=0),
    )(lead)


def second_kernel(schur_ref, own_ref, hi_ref, lo_ref, cols_ref, work, *scratch):
    factor_refs, (send_sem, recv_sem) = scratch[:5], scratch[5:]
    row, col = lax.axis_index("row"), lax.axis_index("col")
    rows_n, cols_n = lax.axis_size("row"), lax.axis_size("col")
    z, core = row // 2, row % 2
    flat, from_flat = row * cols_n + col, col * rows_n + row
    to_row, to_col = flat % rows_n, flat // rows_n
    moves = (to_row != row) | (to_col != col)
    barrier = greet()

    @pl.when(moves)
    def _():
        for peer in ((to_row, to_col), (from_flat // cols_n, from_flat % cols_n)):
            pl.semaphore_signal(barrier, inc=1, device_id=peer, device_id_type=MESH)

    work[...] = schur_ref[...]

    def shift():
        return pltpu.make_async_remote_copy(
            src_ref=own_ref,
            dst_ref=cols_ref.at[to_row // 2, to_row % 2],
            send_sem=send_sem.at[15],
            recv_sem=recv_sem.at[15],
            device_id=(to_row, to_col),
            device_id_type=MESH,
        )

    @pl.when(moves)
    def _():
        pl.semaphore_wait(barrier, 5)
        shift().start()

    @pl.when(jnp.logical_not(moves))
    def _():
        pl.semaphore_wait(barrier, 3)
        cols_ref[z, core] = own_ref[...]

    ring = Ring(lambda b, c: cols_ref.at[b, c], send_sem, recv_sem)
    later = ring.advance_at((4, 5, 6, 7))

    def before(j):
        @pl.when((j == 3) & moves)
        def _():
            shift().wait_recv()

        @pl.when(j == 3)
        def _():
            ring.begin()

        later(j)

    invert_in_place(work, *factor_refs, before=before)
    hi, lo = split(work[...])
    hi_ref[...] = hi
    lo_ref[...] = lo
    ring.finish()

    @pl.when(moves)
    def _():
        shift().wait_send()


def second_factor(schur, own):
    n = schur.shape[0]
    vmem = pl.BlockSpec(memory_space=pltpu.VMEM)
    shapes = [(n, n), (n, n), (ZS, 2, *own.shape)]
    return pl.pallas_call(
        second_kernel,
        out_shape=[jax.ShapeDtypeStruct(s, BF16) for s in shapes],
        in_specs=[vmem] * 2,
        out_specs=[vmem] * 3,
        scratch_shapes=[
            pltpu.VMEM((n, n), F32),
            *factor_scratch(n),
            pltpu.SemaphoreType.DMA((16,)),
            pltpu.SemaphoreType.DMA((16,)),
        ],
        compiler_params=pltpu.CompilerParams(
            vmem_limit_bytes=48 << 20, collective_id=1, has_side_effects=True
        ),
        cost_estimate=pl.CostEstimate(flops=4_000_000_000, bytes_accessed=8 << 20, transcendentals=0),
    )(schur, own)


def on_device(lead, panel, row_present, trailing):
    half = lead.shape[2] // 2
    rows_n, cols_n = lax.axis_size("row"), lax.axis_size("col")
    row_id, col_id = lax.axis_index("row"), lax.axis_index("col")
    count = panel.shape[0]
    first_row = (row_id * cols_n + col_id) * count
    tile_of = (first_row + jnp.arange(count, dtype=jnp.int32)) // TILE
    hits = tile_of[:, None] == jnp.arange(row_present.shape[0], dtype=jnp.int32)[None, :]
    present = jnp.sum(jnp.where(hits, row_present[None, :], 0), axis=1).astype(F32)
    masked = panel * present[:, None]
    hi, lo = split_outside(masked)
    four = [hi[:, :half], lo[:, :half], hi[:, half:], lo[:, half:]]
    row_pieces = lax.all_gather(jnp.stack(four), "col", axis=1, tiled=True)
    *x1_parts, coupling, schur = lead_factor(lead)
    *x2_parts, col_pieces = second_factor(schur, jnp.concatenate(four, axis=0))
    col_pieces = col_pieces.reshape(rows_n, 4, count, half)
    col_parts = [col_pieces[:, n].reshape(rows_n * count, half) for n in range(4)]

    def solve(left_hi, left_lo, right_hi, right_lo):
        first = dot3((left_hi, left_lo), x1_parts, NT).astype(BF16)
        whole = right_hi.astype(F32) + right_lo.astype(F32)
        rest = split_outside(whole - dot(first, coupling, NT))
        second = dot3(rest, x2_parts, NT).astype(BF16)
        return jnp.concatenate([first, second], axis=1)

    rows_all = solve(*[row_pieces[n] for n in range(4)])
    cols_all = solve(*col_parts)
    updated = trailing - dot(rows_all, cols_all, NT)
    factor_rows = lax.dynamic_slice_in_dim(rows_all, col_id * count, count, 0)
    return (updated, factor_rows)


def solution(mesh):
    in_specs = (P(None, "row", None), P(("row", "col"), None), P(), P("row", "col"))
    out_specs = (P("row", "col"), P(("row", "col"), None))
    return jax.shard_map(
        on_device, mesh=mesh, in_specs=in_specs, out_specs=out_specs, check_vma=False
    )
```

```python
import jax
import jax.numpy as jnp
from jax import lax
from jax.experimental import pallas as pl
from jax.experimental.pallas import tpu as pltpu
from jax.sharding import PartitionSpec as P

TILE = 128
F32 = jnp.float32
BF16 = jnp.bfloat16


def lane_cast(x, c):
    return jnp.broadcast_to(x[:, c : c + 1], (8, 128))


def sub_cast(x, j):
    return jnp.broadcast_to(x[j : j + 1, :], (8, 128))


def tree(xs):
    while len(xs) > 1:
        xs = [xs[i] + xs[i + 1] if i + 1 < len(xs) else xs[i] for i in range(0, len(xs), 2)]
    return xs[0]


def factor128(rows):
    lane = lax.broadcasted_iota(jnp.int32, (8, 128), 1)
    sub = lax.broadcasted_iota(jnp.int32, (8, 128), 0)
    zero = jnp.zeros((8, 128), F32)
    rows = list(rows)
    out = []
    for k in range(0, 16, 2):
        c0 = 8 * k
        inside = (lane >= c0) & (lane < c0 + 16)
        casts = {r: [lane_cast(rows[r], c0 + c) for c in range(16)] for r in range(k, min(16, k + 4))}
        cols = [[casts[k][c], casts[k + 1][c]] for c in range(16)]
        forward = [jnp.where(inside, jnp.where(lane - c0 - 8 * i == sub, 1.0, 0.0), rows[k + i]) for i in range(2)]
        full = list(forward)
        recips = [zero, zero]
        for j in range(16):
            at, js = j // 8, j % 8
            recip = 1.0 / sub_cast(cols[j][at], js)
            mult = [cols[j][i] * recip for i in range(2)]
            below = [jnp.where(sub > js, mult[i], 0.0) if i == at else mult[i] for i in range(2)]
            mult[at] = jnp.where(sub == js, 0.0, mult[at])
            for c in range(j + 1, 16):
                pivot = sub_cast(cols[c][at], js)
                cols[c] = [cols[c][i] - mult[i] * pivot for i in range(2)]
            pivot = sub_cast(full[at], js)
            full = [full[i] - mult[i] * pivot for i in range(2)]
            pivot = sub_cast(forward[at], js)
            forward = [forward[i] - below[i] * pivot if i >= at else forward[i] for i in range(2)]
            recips[at] = jnp.where(sub == js, recip, recips[at])
        full = [full[i] * recips[i] for i in range(2)]
        for i in range(2):
            out.append(jnp.where(lane < c0 + 8 * i + 8, forward[i] * lax.sqrt(recips[i]), 0.0))
        pivots = [sub_cast(full[c // 8], c % 8) for c in range(16)]
        far = range(k + 4, 16)
        if len(far) > 0:
            step = split(jnp.concatenate([full[r - k] if k <= r < k + 2 else zero for r in range(16)], axis=0))
            take = dot3(split(jnp.concatenate([jnp.where(inside, rows[r], 0.0) for r in far], axis=0)), step, NN)
        for r in range(k + 2, 16):
            kept = jnp.where(inside, 0.0, rows[r])
            if r < k + 4:
                rows[r] = kept - tree([casts[r][c] * pivots[c] for c in range(16)])
            else:
                rows[r] = kept - take[8 * (r - k - 4) : 8 * (r - k - 4) + 8, :]
    return out


def split(x):
    hi = x.astype(BF16)
    return hi, (x - hi.astype(F32)).astype(BF16)


def split_outside(x):
    hi = lax.reduce_precision(x, 8, 7)
    return hi.astype(BF16), (x - hi).astype(BF16)


NN = (((1,), (0,)), ((), ()))
NT = (((1,), (1,)), ((), ()))


def dot(a, b, dims):
    return lax.dot_general(a, b, dims, preferred_element_type=F32)


def dot3(a, b, dims):
    return dot(a[0], b[0], dims) + (dot(a[0], b[1], dims) + dot(a[1], b[0], dims))


def invert_in_place(x_ref, inv_ref, top_hi, top_lo, left_hi, left_lo, before=None):
    n = x_ref.shape[0]
    blocks = n // 128
    column = lax.broadcasted_iota(jnp.int32, (128, n), 1)

    def step(j, carry):
        if before is not None:
            before(j)
        r0 = pl.multiple_of(j * 128, 128)
        here = pl.ds(r0, 128)
        rows = [x_ref[pl.ds(r0 + 8 * k, 8), here] for k in range(16)]
        for k, row in enumerate(factor128(rows)):
            inv_ref[8 * k : 8 * k + 8, :] = row
        inv = inv_ref[...]
        inv_parts = split(inv)
        top = dot3(inv_parts, split(x_ref[here, :]), NN)
        hi, lo = split(top)
        top_hi[...] = hi
        top_lo[...] = lo
        inv_hi, inv_lo = inv_parts
        top_hi[:, here] = inv_hi
        top_lo[:, here] = inv_lo
        left = dot3(split(x_ref[:, here]), inv_parts, NT)
        hi, lo = split(left)
        left_hi[...] = hi
        left_lo[...] = lo
        x_ref[here, :] = jnp.where(column < r0, top, 0.0)
        x_ref[here, here] = inv

        def below(i, inner):
            i0 = pl.multiple_of(i * 128, 128)
            at = pl.ds(i0, 128)
            take = dot3((left_hi[at, :], left_lo[at, :]), (top_hi[...], top_lo[...]), NN)
            x_ref[at, here] = jnp.zeros((128, 128), F32)
            x_ref[at, :] = x_ref[at, :] - take
            return inner

        lax.fori_loop(j + 1, blocks, below, 0)
        return carry

    lax.fori_loop(0, blocks, step, 0)


def factor_scratch(n):
    return [
        pltpu.VMEM((128, 128), F32),
        pltpu.VMEM((128, n), BF16),
        pltpu.VMEM((128, n), BF16),
        pltpu.VMEM((n, 128), BF16),
        pltpu.VMEM((n, 128), BF16),
    ]


ZS = 8
MESH = pl.DeviceIdType.MESH


def neighbours():
    row, col = lax.axis_index("row"), lax.axis_index("col")
    z, core = row // 2, row % 2
    up = (lax.rem(z + 1, ZS) * 2 + core, col)
    down = (lax.rem(z + ZS - 1, ZS) * 2 + core, col)
    return z, core, up, down, (z * 2 + 1 - core, col)


class Ring:
    def __init__(self, block_of, send_sem, recv_sem):
        z, core, up, down, other = neighbours()

        def copy(n, block, peer):
            part = block_of(lax.rem(block + ZS, ZS), core)
            return pltpu.make_async_remote_copy(
                src_ref=part,
                dst_ref=part,
                send_sem=send_sem.at[n],
                recv_sem=recv_sem.at[n],
                device_id=peer,
                device_id_type=MESH,
            )

        self.ups = [copy(n, z - n, up) for n in range(4)]
        self.downs = [copy(4 + n, z + n, down) for n in range(3)]
        self.across = [copy(7 + n, z - n, other) for n in range(5)]
        self.across += [copy(11 + n, z + n, other) for n in range(1, 4)]

    def begin(self):
        self.ups[0].start()
        self.downs[0].start()
        self.across[0].start()

    def advance(self, n):
        self.ups[n].wait_recv()
        if n < 3:
            self.ups[n + 1].start()
            self.downs[n].wait_recv()
        if n < 2:
            self.downs[n + 1].start()
        self.across[1 + n].start()
        if n < 3:
            self.across[5 + n].start()

    def finish(self):
        for c in self.across:
            c.wait()
        for c in self.ups + self.downs:
            c.wait_send()

    def advance_at(self, turns):
        def before(j):
            for n, turn in enumerate(turns):

                @pl.when(j == turn)
                def _():
                    self.advance(n)

        return before


def greet():
    barrier = pltpu.get_barrier_semaphore()
    for peer in neighbours()[2:]:
        pl.semaphore_signal(barrier, inc=1, device_id=peer, device_id_type=MESH)
    return barrier


def lead_kernel(lead_ref, hi_ref, lo_ref, coupling_ref, schur_ref, buf, work, *scratch):
    factor_refs, (send_sem, recv_sem) = scratch[:5], scratch[5:]
    z, core = neighbours()[:2]
    half = lead_ref.shape[2] // 2
    barrier = greet()
    buf[0, z, core] = lead_ref[0, :, :half]
    buf[1, z, core] = lead_ref[1, :, :half]
    buf[2, z, core] = lead_ref[1, :, half:]
    pl.semaphore_wait(barrier, 3)

    first = Ring(lambda b, c: buf.at[pl.ds(0, 1), b, c], send_sem.at[0], recv_sem.at[0])
    rest = Ring(lambda b, c: buf.at[pl.ds(1, 2), b, c], send_sem.at[1], recv_sem.at[1])
    first.begin()
    for n in range(4):
        first.advance(n)
    rest.begin()
    first.finish()
    work[...] = buf[0].reshape(work.shape).astype(F32)
    invert_in_place(work, *factor_refs, before=rest.advance_at((2, 4, 5, 7)))
    hi, lo = split(work[...])
    hi_ref[...] = hi
    lo_ref[...] = lo
    rest.finish()

    wide = 256
    for n in range(half // wide):
        at = slice(n * wide, n * wide + wide)
        depth = (n + 1) * wide
        left = buf[1, :, :, :, :depth].reshape(half, depth)
        coupling_ref[:, at] = (dot(left, hi_ref[at, :depth], NT) + dot(left, lo_ref[at, :depth], NT)).astype(BF16)

    def schur_columns(n, carry):
        at = pl.ds(pl.multiple_of(n * wide, wide), wide)
        block = buf[2, :, :, :, at].reshape(half, wide).astype(F32)
        schur_ref[:, at] = block - dot(coupling_ref[...], coupling_ref[at, :], NT)
        return carry

    lax.fori_loop(0, half // wide, schur_columns, 0)


def lead_factor(lead):
    half = lead.shape[2] // 2
    square = (half, half)
    vmem = pl.BlockSpec(memory_space=pltpu.VMEM)
    shapes = [(square, BF16)] * 3 + [(square, F32)]
    return pl.pallas_call(
        lead_kernel,
        out_shape=[jax.ShapeDtypeStruct(s, t) for s, t in shapes],
        in_specs=[vmem],
        out_specs=[vmem] * 4,
        scratch_shapes=[
            pltpu.VMEM((3, ZS, 2, half // 16, half), BF16),
            pltpu.VMEM(square, F32),
            *factor_scratch(half),
            pltpu.SemaphoreType.DMA((2, 15)),
            pltpu.SemaphoreType.DMA((2, 15)),
        ],
        compiler_params=pltpu.CompilerParams(
            vmem_limit_bytes=48 << 20, collective_id=0, has_side_effects=True
        ),
        cost_estimate=pl.CostEstimate(flops=6_000_000_000, bytes_accessed=16 << 20, transcendentals=0),
    )(lead)


def second_kernel(schur_ref, own_ref, hi_ref, lo_ref, cols_ref, work, *scratch):
    factor_refs, (send_sem, recv_sem) = scratch[:5], scratch[5:]
    row, col = lax.axis_index("row"), lax.axis_index("col")
    rows_n, cols_n = lax.axis_size("row"), lax.axis_size("col")
    z, core = row // 2, row % 2
    flat, from_flat = row * cols_n + col, col * rows_n + row
    to_row, to_col = flat % rows_n, flat // rows_n
    moves = (to_row != row) | (to_col != col)
    barrier = greet()

    @pl.when(moves)
    def _():
        for peer in ((to_row, to_col), (from_flat // cols_n, from_flat % cols_n)):
            pl.semaphore_signal(barrier, inc=1, device_id=peer, device_id_type=MESH)

    work[...] = schur_ref[...]

    def shift():
        return pltpu.make_async_remote_copy(
            src_ref=own_ref,
            dst_ref=cols_ref.at[to_row // 2, to_row % 2],
            send_sem=send_sem.at[15],
            recv_sem=recv_sem.at[15],
            device_id=(to_row, to_col),
            device_id_type=MESH,
        )

    @pl.when(moves)
    def _():
        pl.semaphore_wait(barrier, 5)
        shift().start()

    @pl.when(jnp.logical_not(moves))
    def _():
        pl.semaphore_wait(barrier, 3)
        cols_ref[z, core] = own_ref[...]

    ring = Ring(lambda b, c: cols_ref.at[b, c], send_sem, recv_sem)
    later = ring.advance_at((3, 4, 5, 6))

    def before(j):
        @pl.when((j == 2) & moves)
        def _():
            shift().wait_recv()

        @pl.when(j == 2)
        def _():
            ring.begin()

        later(j)

    invert_in_place(work, *factor_refs, before=before)
    hi, lo = split(work[...])
    hi_ref[...] = hi
    lo_ref[...] = lo
    ring.finish()

    @pl.when(moves)
    def _():
        shift().wait_send()


def second_factor(schur, own):
    n = schur.shape[0]
    vmem = pl.BlockSpec(memory_space=pltpu.VMEM)
    shapes = [(n, n), (n, n), (ZS, 2, *own.shape)]
    return pl.pallas_call(
        second_kernel,
        out_shape=[jax.ShapeDtypeStruct(s, BF16) for s in shapes],
        in_specs=[vmem] * 2,
        out_specs=[vmem] * 3,
        scratch_shapes=[
            pltpu.VMEM((n, n), F32),
            *factor_scratch(n),
            pltpu.SemaphoreType.DMA((16,)),
            pltpu.SemaphoreType.DMA((16,)),
        ],
        compiler_params=pltpu.CompilerParams(
            vmem_limit_bytes=48 << 20, collective_id=1, has_side_effects=True
        ),
        cost_estimate=pl.CostEstimate(flops=4_000_000_000, bytes_accessed=8 << 20, transcendentals=0),
    )(schur, own)


def on_device(lead, panel, row_present, trailing):
    half = lead.shape[2] // 2
    rows_n, cols_n = lax.axis_size("row"), lax.axis_size("col")
    row_id, col_id = lax.axis_index("row"), lax.axis_index("col")
    count = panel.shape[0]
    first_row = (row_id * cols_n + col_id) * count
    tile_of = (first_row + jnp.arange(count, dtype=jnp.int32)) // TILE
    hits = tile_of[:, None] == jnp.arange(row_present.shape[0], dtype=jnp.int32)[None, :]
    present = jnp.sum(jnp.where(hits, row_present[None, :], 0), axis=1).astype(F32)
    masked = panel * present[:, None]
    hi, lo = split_outside(masked)
    four = [hi[:, :half], lo[:, :half], hi[:, half:], lo[:, half:]]
    row_pieces = lax.all_gather(jnp.stack(four), "col", axis=1, tiled=True)
    *x1_parts, coupling, schur = lead_factor(lead)
    *x2_parts, col_pieces = second_factor(schur, jnp.concatenate(four, axis=0))
    col_pieces = col_pieces.reshape(rows_n, 4, count, half)
    col_parts = [col_pieces[:, n].reshape(rows_n * count, half) for n in range(4)]

    def solve(left_hi, left_lo, right_hi, right_lo):
        first = dot3((left_hi, left_lo), x1_parts, NT).astype(BF16)
        whole = right_hi.astype(F32) + right_lo.astype(F32)
        rest = split_outside(whole - dot(first, coupling, NT))
        second = dot3(rest, x2_parts, NT).astype(BF16)
        return jnp.concatenate([first, second], axis=1)

    rows_all = solve(*[row_pieces[n] for n in range(4)])
    cols_all = solve(*col_parts)
    updated = trailing - dot(rows_all, cols_all, NT)
    factor_rows = lax.dynamic_slice_in_dim(rows_all, col_id * count, count, 0)
    return (updated, factor_rows)


def solution(mesh):
    in_specs = (P(None, "row", None), P(("row", "col"), None), P(), P("row", "col"))
    out_specs = (P("row", "col"), P(("row", "col"), None))
    return jax.shard_map(
        on_device, mesh=mesh, in_specs=in_specs, out_specs=out_specs, check_vma=False
    )
```
